1024 devices in a mesh: head: 8 (over y), inner: 8 (over z_hi, core), outer: 16 (over z_lo, x).
Axes of the slice: x: 8, y: 8, z: 8 (z_hi: 4, z_lo: 2; z = z_hi * 2 + z_lo), core: 2. Of those that a mesh axis runs over, the one named last changes fastest.
Arguments:
- queries: bfloat16 [49152, 8192], P(('inner', 'outer', 'head')), may hold values from -30 to 30
- keys: bfloat16 [49152, 1024], P(('inner', 'outer', 'head')), may hold values from -30 to 30
- values: bfloat16 [49152, 1024], P(('inner', 'outer', 'head')), may hold values from -6 to 6
- positions: int32 [49152], replicated, may hold values from 0 to 49151, as said below
- plan: int32 [128, 3], replicated, may hold values 0 or 1
Outputs:
- attention: bfloat16 [49152, 8192], P(('inner', 'outer', 'head'))
- log_sum: float32 [64, 49152], P('head', ('inner', 'outer'))
The draws below stay inside these ranges and needn't reach their ends.
Inputs may be any that keep to these rules, and one draw needn't show every extreme that they name: Every position 0 to 49151 appears once; each aligned run of 192 rows holds consecutive positions in increasing order.
All inputs are finite; a program needn't handle non-finite values.
Results may differ from the reference program's by a relative error of at most 0.0039.
Values may be sent and summed in bfloat16 or wider, within the bound.
A program may use at most 32 MiB of HBM per device.

```python
import jax
import jax.numpy as jnp
from jax import lax

QUERY_HEADS = 64
KEY_VALUE_HEADS = 8
HEAD_WIDTH = 128
GROUP = 8
BLOCK_TOKENS = 384
CYCLE = 8
CYCLES = 16
BLOCKS = 128
SEQUENCE_TOKENS = 49152


def draw_queries(key, part):
    base_index = jax.random.normal(jax.random.fold_in(key, 21), (SEQUENCE_TOKENS, QUERY_HEADS, HEAD_WIDTH), jnp.float32)
    return base_index.reshape(SEQUENCE_TOKENS, QUERY_HEADS * HEAD_WIDTH).astype(jnp.bfloat16)


def draw_keys(key, part):
    base_index = jax.random.normal(jax.random.fold_in(key, 23), (SEQUENCE_TOKENS, KEY_VALUE_HEADS, HEAD_WIDTH), jnp.float32)
    return base_index.reshape(SEQUENCE_TOKENS, KEY_VALUE_HEADS * HEAD_WIDTH).astype(jnp.bfloat16)


def draw_positions(key, part):
    half = BLOCK_TOKENS // 2
    order = jax.random.permutation(jax.random.fold_in(key, 31), SEQUENCE_TOKENS // half).astype(jnp.int32)
    rows_all = jnp.arange(SEQUENCE_TOKENS, dtype=jnp.int32)
    return order[rows_all // half] * half + rows_all % half


def set_ends(array, own_key, smallest, largest):
    spot = [jax.random.randint(jax.random.fold_in(own_key, axis), (), 0, length) for axis, length in enumerate(array.shape)]
    main_axis = array.shape.index(max(array.shape))
    next_to = spot[:main_axis] + [(spot[main_axis] + 1) % array.shape[main_axis]] + spot[main_axis + 1:]
    return array.at[tuple(spot)].set(smallest).at[tuple(next_to)].set(largest)


def block_levels(own_key, extent, cuts, smallest, top_value):
    level = 1.0
    for dim, parts in cuts:
        heights = jax.random.uniform(jax.random.fold_in(jax.random.fold_in(own_key, 6), dim), (parts,), jnp.float32, smallest / len(cuts), top_value / len(cuts))
        level = level * jnp.repeat(jnp.exp(heights), extent[dim] // parts).reshape((-1,) + (1,) * (len(extent) - 1 - dim))
    return level


def gaussian(key, shape, spread, reach, pieces=(), kind=jnp.bfloat16):
    values = jax.random.normal(key, shape, jnp.float32) * spread
    if len(pieces) > 0:
        values = block_levels(key, shape, pieces, -0.22, 0.18) * values
    return jnp.clip(values, min=-reach, max=reach).astype(kind)


def setup_inputs(seed: int = 0) -> dict:
    key_of = jax.random.split(jax.random.key(seed), 6)
    queries = draw_queries(jax.random.fold_in(key_of[5], 71), 0)
    keys = draw_keys(jax.random.fold_in(key_of[5], 71), 0)
    values = gaussian(key_of[2], (SEQUENCE_TOKENS, KEY_VALUE_HEADS * HEAD_WIDTH), 1.0, 6.0, ((0, 1024),))
    positions = draw_positions(jax.random.fold_in(key_of[5], 71), 0)
    plan = set_ends((jax.random.randint(key_of[4], (BLOCKS, 3), 0, 4) < 3).astype(jnp.int32), jax.random.fold_in(key_of[4], 1), 0, 1)
    return {"queries": queries, "keys": keys, "values": values, "positions": positions, "plan": plan}


def key_blocks(here, inner_count, outer_count):
    inner_here = here // outer_count
    outer_here = here % outer_count
    first = ((inner_here - 1) % inner_count) * outer_count + outer_here
    second = ((inner_here - 2) % inner_count) * outer_count + outer_here
    third = inner_here * outer_count + (outer_here - 1) % outer_count
    return (here, first, second, third)


def visible_mask(positions, plan, sources, here, block_rows):
    table = positions.reshape(-1, block_rows)
    query_place = table[here]
    key_place = jnp.concatenate([table[source] for source in sources])
    flags = jnp.concatenate([jnp.ones((1,), jnp.int32), plan[here]])
    step_used = jnp.repeat(flags, block_rows)
    return (key_place[None, :] <= query_place[:, None]) & (step_used[None, :] == 1)


def attend_window(query_head_stack, key_head_stack, value_head_stack, causal_mask, group, head_size):
    def one_head(index):
        query_now = query_head_stack[index]
        key_now = key_head_stack[index // group]
        value_now = value_head_stack[index // group]
        scores = lax.dot_general(query_now, key_now, (((1,), (1,)), ((), ())), preferred_element_type=jnp.float32)
        scores = scores * (head_size ** -0.5)
        scores = jnp.where(causal_mask, scores, -jnp.inf)
        top = jnp.max(scores, axis=1, keepdims=True)
        weights = jnp.exp(scores - top)
        total = jnp.sum(weights, axis=1, keepdims=True)
        mixed_output = jnp.dot(weights.astype(jnp.bfloat16), value_now, preferred_element_type=jnp.float32)
        return (mixed_output / total).astype(jnp.bfloat16), (top + jnp.log(total))[:, 0]
    return lax.map(one_head, jnp.arange(query_head_stack.shape[0], dtype=jnp.int32))


def reference(queries, keys, values, positions, plan):
    def one_block(here):
        sources = key_blocks(here, CYCLE, CYCLES)
        causal_mask = visible_mask(positions, plan, sources, here, BLOCK_TOKENS)
        start = (here * BLOCK_TOKENS).astype(jnp.int32)
        query_head_stack = lax.dynamic_slice_in_dim(queries, start, BLOCK_TOKENS, 0).reshape(BLOCK_TOKENS, QUERY_HEADS, HEAD_WIDTH).transpose(1, 0, 2)
        key_row_list = jnp.concatenate([lax.dynamic_slice_in_dim(keys, (source * BLOCK_TOKENS).astype(jnp.int32), BLOCK_TOKENS, 0) for source in sources])
        value_row_list = jnp.concatenate([lax.dynamic_slice_in_dim(values, (source * BLOCK_TOKENS).astype(jnp.int32), BLOCK_TOKENS, 0) for source in sources])
        key_head_stack = key_row_list.reshape(4 * BLOCK_TOKENS, KEY_VALUE_HEADS, HEAD_WIDTH).transpose(1, 0, 2)
        value_head_stack = value_row_list.reshape(4 * BLOCK_TOKENS, KEY_VALUE_HEADS, HEAD_WIDTH).transpose(1, 0, 2)
        mixed_output, hidden_states = attend_window(query_head_stack, key_head_stack, value_head_stack, causal_mask, GROUP, HEAD_WIDTH)
        return mixed_output.transpose(1, 0, 2).reshape(BLOCK_TOKENS, QUERY_HEADS * HEAD_WIDTH), hidden_states
    mixed_output, hidden_states = lax.map(one_block, jnp.arange(BLOCKS, dtype=jnp.int32))
    return mixed_output.reshape(SEQUENCE_TOKENS, QUERY_HEADS * HEAD_WIDTH), hidden_states.transpose(1, 0, 2).reshape(QUERY_HEADS, SEQUENCE_TOKENS)
```

```python
import functools

import jax
import jax.numpy as jnp
from jax import lax
from jax.experimental import pallas as pl
from jax.experimental.pallas import tpu as pltpu
from jax.sharding import PartitionSpec as P

WIDTH = 128
GROUP = 8
STEPS = 4
LANES = 128
CHUNK_HEADS = 2
EARLY_CHUNKS = 2
QUERY_TILE = 128
MASKED = -1e30
MESH = pl.DeviceIdType.MESH


def attention_kernel(
    sizes,
    q_ref,
    k_ref,
    v_ref,
    place_ref,
    plan_ref,
    out_ref,
    log_ref,
    keys,
    values,
    q_buf,
    o_buf,
    bias,
    logs,
    place,
    plan,
    local_sem,
    kv_send,
    kv_recv,
    next_send,
    next_recv,
    q_send,
    q_recv,
    o_send,
    o_recv,
):
    heads, inners, outers = sizes
    rows = q_ref.shape[0]
    block_rows = rows * heads
    run = block_rows // 2
    chunks = GROUP // CHUNK_HEADS
    wide = CHUNK_HEADS * WIDTH
    me = lax.axis_index("head")
    inner = lax.axis_index("inner")
    outer = lax.axis_index("outer")
    offsets = sorted(range(1, heads), key=lambda r: -min(r, heads - r))

    def peer(r):
        return lax.rem(me + r, heads)

    def row_span(owner):
        return pl.ds(pl.multiple_of(owner * rows, 16), rows)

    targets = (
        {"inner": lax.rem(inner + 1, inners)},
        {"inner": lax.rem(inner + 2, inners)},
        {"outer": lax.rem(outer + 1, outers)},
    )
    origins = (
        {"inner": lax.rem(inner + inners - 1, inners)},
        {"inner": lax.rem(inner + inners - 2, inners)},
        {"outer": lax.rem(outer + outers - 1, outers)},
    )

    def kv_copy(which, r):
        ref, buf = ((k_ref, keys), (v_ref, values))[which]
        to = peer(r)
        return pltpu.make_async_remote_copy(
            src_ref=ref.at[:, pl.ds(pl.multiple_of(to * WIDTH, WIDTH), WIDTH)],
            dst_ref=buf.at[0, row_span(me), pl.ds(0, WIDTH)],
            send_sem=kv_send.at[which, r],
            recv_sem=kv_recv.at[which, r],
            device_id={"head": to},
            device_id_type=MESH,
        )

    def kv_landing(which, r):
        buf = (keys, values)[which]
        part = buf.at[0, row_span(lax.rem(me + heads - r, heads)), pl.ds(0, WIDTH)]
        return pltpu.make_async_remote_copy(
            src_ref=part,
            dst_ref=part,
            send_sem=kv_send.at[which, r],
            recv_sem=kv_recv.at[which, r],
            device_id={"head": peer(r)},
            device_id_type=MESH,
        )

    def next_copy(which, step):
        buf = (keys, values)[which]
        return pltpu.make_async_remote_copy(
            src_ref=buf.at[0, :, pl.ds(0, WIDTH)],
            dst_ref=buf.at[step + 1, :, pl.ds(0, WIDTH)],
            send_sem=next_send.at[which, step],
            recv_sem=next_recv.at[which, step],
            device_id=targets[step],
            device_id_type=MESH,
        )

    def q_columns(owner, c):
        return pl.ds(pl.multiple_of(owner * (GROUP * WIDTH) + c * wide, WIDTH), wide)

    def q_copy(c, r):
        to = peer(r)
        return pltpu.make_async_remote_copy(
            src_ref=q_ref.at[:, q_columns(to, c)],
            dst_ref=q_buf.at[c, row_span(me)],
            send_sem=q_send.at[c, r],
            recv_sem=q_recv.at[c, r],
            device_id={"head": to},
            device_id_type=MESH,
        )

    def q_landing(c, r):
        part = q_buf.at[c, row_span(lax.rem(me + heads - r, heads))]
        return pltpu.make_async_remote_copy(
            src_ref=part,
            dst_ref=part,
            send_sem=q_send.at[c, r],
            recv_sem=q_recv.at[c, r],
            device_id={"head": peer(r)},
            device_id_type=MESH,
        )

    def o_copy(c, r):
        to = peer(r)
        return pltpu.make_async_remote_copy(
            src_ref=o_buf.at[c, row_span(to)],
            dst_ref=out_ref.at[:, q_columns(me, c)],
            send_sem=o_send.at[c, r],
            recv_sem=o_recv.at[c, r],
            device_id={"head": to},
            device_id_type=MESH,
        )

    def o_landing(c, r):
        part = out_ref.at[:, q_columns(lax.rem(me + heads - r, heads), c)]
        return pltpu.make_async_remote_copy(
            src_ref=part,
            dst_ref=part,
            send_sem=o_send.at[c, r],
            recv_sem=o_recv.at[c, r],
            device_id={"head": peer(r)},
            device_id_type=MESH,
        )

    own_kv = [
        pltpu.make_async_copy(
            ref.at[:, pl.ds(pl.multiple_of(me * WIDTH, WIDTH), WIDTH)],
            buf.at[0, row_span(me), pl.ds(0, WIDTH)],
            local_sem.at[n],
        )
        for n, (ref, buf) in enumerate(((k_ref, keys), (v_ref, values)))
    ]
    tables = [
        pltpu.make_async_copy(place_ref, place, local_sem.at[2]),
        pltpu.make_async_copy(plan_ref, plan, local_sem.at[3]),
    ]

    def own_q(c):
        return pltpu.make_async_copy(
            q_ref.at[:, q_columns(me, c)], q_buf.at[c, row_span(me)], q_send.at[c, 0]
        )

    def own_o(c):
        return pltpu.make_async_copy(
            o_buf.at[c, row_span(me)], out_ref.at[:, q_columns(me, c)], o_send.at[c, 0]
        )

    barrier = pltpu.get_barrier_semaphore()
    for r in offsets:
        pl.semaphore_signal(barrier, inc=1, device_id={"head": peer(r)}, device_id_type=MESH)
    for origin in origins:
        pl.semaphore_signal(barrier, inc=1, device_id=origin, device_id_type=MESH)
    for copy in own_kv + tables:
        copy.start()
    for c in range(chunks):
        own_q(c).start()
    pl.semaphore_wait(barrier, len(offsets) + len(origins))

    for r in offsets:
        kv_copy(0, r).start()
        kv_copy(1, r).start()
    for c in range(EARLY_CHUNKS):
        for r in offsets:
            q_copy(c, r).start()

    for copy in tables:
        copy.wait()
    here = inner * outers + outer
    sources = (
        here,
        lax.rem(inner + inners - 1, inners) * outers + outer,
        lax.rem(inner + inners - 2, inners) * outers + outer,
        inner * outers + lax.rem(outer + outers - 1, outers),
    )
    def starts(block):
        first = block * block_rows
        second = first + run
        out = []
        for spot in (first, second):
            line = place[pl.ds(lax.div(spot, LANES), 1), :]
            lane = lax.broadcasted_iota(jnp.int32, (1, LANES), 1)
            out.append(
                jnp.sum(
                    jnp.where(lane == lax.rem(spot, LANES), line, 0), axis=1, keepdims=True
                )
            )
        return out

    lane = lax.broadcasted_iota(jnp.int32, plan.shape, 1)
    used = jnp.max(jnp.where(lane == here, plan[...], 0), axis=1, keepdims=True)
    q_first, q_second = starts(here)
    q_row = lax.broadcasted_iota(jnp.int32, (block_rows, 1), 0)
    q_place = jnp.where(q_row < run, q_first + q_row, q_second + q_row - run)
    k_row = lax.broadcasted_iota(jnp.int32, (1, block_rows), 1)
    for step, source in enumerate(sources):
        k_first, k_second = starts(source)
        k_place = jnp.where(k_row < run, k_first + k_row, k_second + k_row - run)
        if step:
            k_place = jnp.where(used[step - 1 : step] == 1, k_place, jnp.int32(2**30))
        bias[:, step * block_rows : (step + 1) * block_rows] = jnp.where(
            k_place <= q_place, jnp.float32(0), jnp.float32(MASKED)
        )
    values[:, :, WIDTH:] = jnp.ones((STEPS, block_rows, LANES), values.dtype)
    logs[...] = jnp.zeros_like(logs)

    for which in range(2):
        own_kv[which].wait()
        for r in offsets:
            kv_landing(which, r).wait_recv()
        for step in range(STEPS - 1):
            next_copy(which, step).start()
    for c in range(EARLY_CHUNKS, chunks):
        for r in offsets:
            q_copy(c, r).start()
    for which in range(2):
        for step in range(STEPS - 1):
            next_copy(which, step).wait_recv()

    scale = WIDTH**-0.5
    exponent = scale * 1.4426950408889634

    def one_chunk(c, carry):
        own_q(c).wait()
        for r in offsets:
            q_landing(c, r).wait_recv()
        for j in range(CHUNK_HEADS):
            columns = slice(j * WIDTH, (j + 1) * WIDTH)
            for tile in range(0, block_rows, QUERY_TILE):
                span = slice(tile, tile + QUERY_TILE)
                query = q_buf[c, span, columns]
                scores = [
                    lax.dot_general(
                        query,
                        keys[step],
                        (((1,), (1,)), ((), ())),
                        preferred_element_type=jnp.float32,
                    )
                    + bias[span, step * block_rows : (step + 1) * block_rows]
                    for step in range(STEPS)
                ]
                top = functools.reduce(jnp.maximum, scores)
                top = jnp.max(top, axis=1, keepdims=True)
                mixed = jnp.zeros((QUERY_TILE, 2 * WIDTH), jnp.float32)
                for step in range(STEPS):
                    weights = jnp.exp2((scores[step] - top) * exponent)
                    mixed += jnp.dot(
                        weights.astype(jnp.bfloat16),
                        values[step],
                        preferred_element_type=jnp.float32,
                    )
                total = mixed[:, WIDTH:]
                o_buf[c, span, columns] = (mixed[:, :WIDTH] / total).astype(o_buf.dtype)
                lane = lax.broadcasted_iota(jnp.int32, (QUERY_TILE, LANES), 1)
                logs[span, :] = jnp.where(
                    lane == c * CHUNK_HEADS + j, top * scale + jnp.log(total), logs[span, :]
                )
        own_o(c).start()
        for r in offsets:
            o_copy(c, r).start()
        return carry

    lax.fori_loop(0, chunks, one_chunk, 0)
    log_ref[...] = jnp.transpose(logs[...])[:GROUP]

    for which in range(2):
        for r in offsets:
            kv_copy(which, r).wait_send()
        for step in range(STEPS - 1):
            next_copy(which, step).wait_send()
    for c in range(chunks):
        own_o(c).wait()
        for r in offsets:
            q_copy(c, r).wait_send()
            o_copy(c, r).wait_send()
            o_landing(c, r).wait_recv()


def per_device(queries, keys, values, positions, plan):
    sizes = tuple(lax.axis_size(name) for name in ("head", "inner", "outer"))
    heads = sizes[0]
    rows = queries.shape[0]
    block_rows = rows * heads
    chunks = GROUP // CHUNK_HEADS
    place = positions.reshape(-1, LANES)
    used = plan.T
    anywhere = pl.BlockSpec(memory_space=pl.ANY)
    dma = pltpu.SemaphoreType.DMA
    kind = queries.dtype
    return pl.pallas_call(
        functools.partial(attention_kernel, sizes),
        out_shape=(
            jax.ShapeDtypeStruct(queries.shape, kind),
            jax.ShapeDtypeStruct((GROUP, block_rows), jnp.float32),
        ),
        in_specs=[anywhere] * 5,
        out_specs=(anywhere, pl.BlockSpec(memory_space=pltpu.VMEM)),
        scratch_shapes=[
            pltpu.VMEM((STEPS, block_rows, WIDTH), kind),
            pltpu.VMEM((STEPS, block_rows, 2 * WIDTH), kind),
            pltpu.VMEM((chunks, block_rows, CHUNK_HEADS * WIDTH), kind),
            pltpu.VMEM((chunks, block_rows, CHUNK_HEADS * WIDTH), kind),
            pltpu.VMEM((block_rows, STEPS * block_rows), jnp.float32),
            pltpu.VMEM((block_rows, LANES), jnp.float32),
            pltpu.VMEM(place.shape, jnp.int32),
            pltpu.VMEM(used.shape, jnp.int32),
            dma((4,)),
            dma((2, heads)),
            dma((2, heads)),
            dma((2, STEPS - 1)),
            dma((2, STEPS - 1)),
            dma((chunks, heads)),
            dma((chunks, heads)),
            dma((chunks, heads)),
            dma((chunks, heads)),
        ],
        compiler_params=pltpu.CompilerParams(
            collective_id=0, has_side_effects=True, vmem_limit_bytes=40 * 1024 * 1024
        ),
    )(queries, keys, values, place, used)


def solution(mesh):
    rows = P(("inner", "outer", "head"), None)
    return jax.shard_map(
        per_device,
        mesh=mesh,
        in_specs=(rows, rows, rows, P(), P()),
        out_specs=(rows, P("head", ("inner", "outer"))),
        check_vma=False,
    )
```

```python
import functools

import jax
import jax.numpy as jnp
from jax import lax
from jax.experimental import pallas as pl
from jax.experimental.pallas import tpu as pltpu
from jax.sharding import PartitionSpec as P

WIDTH = 128
GROUP = 8
STEPS = 4
LANES = 128
CHUNK_HEADS = 2
EARLY_CHUNKS = 1
QUERY_TILE = 192
MASKED = -1e30
HAND_OVER_PARTS = 3
MESH = pl.DeviceIdType.MESH


def attention_kernel(
    sizes,
    q_ref,
    k_ref,
    v_ref,
    place_ref,
    plan_ref,
    out_ref,
    log_ref,
    kv_buf,
    q_buf,
    o_buf,
    bias,
    logs,
    place,
    plan,
    local_sem,
    kv_send,
    kv_recv,
    next_send,
    next_recv,
    relay_send,
    q_send,
    q_recv,
    o_send,
    o_recv,
):
    heads, inners, outers = sizes
    rows = q_ref.shape[0]
    block_rows = rows * heads
    run = block_rows // 2
    chunks = GROUP // CHUNK_HEADS
    wide = CHUNK_HEADS * WIDTH
    me = lax.axis_index("head")
    inner = lax.axis_index("inner")
    outer = lax.axis_index("outer")
    offsets = sorted(range(1, heads), key=lambda r: -min(r, heads - r))
    pieces = [0] + offsets[::-1]
    side = lax.rem(inner, 2)
    even = side == 0

    def peer(r):
        return lax.rem(me + r, heads)

    def row_span(owner):
        return pl.ds(pl.multiple_of(owner * rows, 16), rows)

    targets = (
        {"inner": lax.rem(inner + 1, inners)},
        {"inner": lax.rem(inner + 2, inners)},
        {"outer": lax.rem(outer + 1, outers)},
    )
    origins = (
        {"inner": lax.rem(inner + inners - 1, inners)},
        {"inner": lax.rem(inner + inners - 2, inners)},
        {"outer": lax.rem(outer + outers - 1, outers)},
    )

    partner = {"inner": inner + 1 - 2 * side}
    key_value = pl.ds(0, WIDTH)

    def kv_copy(which, r):
        ref = (k_ref, v_ref)[which]
        to = peer(r)
        return pltpu.make_async_remote_copy(
            src_ref=ref.at[:, pl.ds(pl.multiple_of(to * WIDTH, WIDTH), WIDTH)],
            dst_ref=kv_buf.at[which, 0, row_span(me), key_value],
            send_sem=kv_send.at[which, r],
            recv_sem=kv_recv.at[which, r],
            device_id={"head": to},
            device_id_type=MESH,
        )

    def piece(which, slot, r):
        return kv_buf.at[which, slot, row_span(lax.rem(me + heads - r, heads)), key_value]

    def kv_landing(which, r):
        part = piece(which, 0, r)
        return pltpu.make_async_remote_copy(
            src_ref=part,
            dst_ref=part,
            send_sem=kv_send.at[which, r],
            recv_sem=kv_recv.at[which, r],
            device_id={"head": peer(r)},
            device_id_type=MESH,
        )

    def next_copy(which, step, r):
        return pltpu.make_async_remote_copy(
            src_ref=piece(which, 0, r),
            dst_ref=piece(which, step + 1, r),
            send_sem=next_send.at[which, step, r],
            recv_sem=next_recv.at[which, step, r],
            device_id=targets[step],
            device_id_type=MESH,
        )

    def next_copies(which, r, act):
        act(next_copy(which, 2, r))
        act(next_copy(which, which, r))

        @pl.when(even)
        def _():
            act(next_copy(which, 1 - which, r))

    def relay_copy(r):
        return pltpu.make_async_remote_copy(
            src_ref=piece(side, 1 + side, r),
            dst_ref=piece(side, 2 - side, r),
            send_sem=relay_send.at[r],
            recv_sem=next_recv.at[side, 1 - side, r],
            device_id=partner,
            device_id_type=MESH,
        )

    def next_landing(which, step, r):
        part = piece(which, step + 1, r)
        return pltpu.make_async_remote_copy(
            src_ref=part,
            dst_ref=part,
            send_sem=relay_send.at[r],
            recv_sem=next_recv.at[which, step, r],
            device_id=partner,
            device_id_type=MESH,
        )

    def q_columns(owner, c):
        return pl.ds(pl.multiple_of(owner * (GROUP * WIDTH) + c * wide, WIDTH), wide)

    def q_copy(c, r):
        to = peer(r)
        return pltpu.make_async_remote_copy(
            src_ref=q_ref.at[:, q_columns(to, c)],
            dst_ref=q_buf.at[c, row_span(me)],
            send_sem=q_send.at[c, r],
            recv_sem=q_recv.at[c, r],
            device_id={"head": to},
            device_id_type=MESH,
        )

    def q_landing(c, r):
        part = q_buf.at[c, row_span(lax.rem(me + heads - r, heads))]
        return pltpu.make_async_remote_copy(
            src_ref=part,
            dst_ref=part,
            send_sem=q_send.at[c, r],
            recv_sem=q_recv.at[c, r],
            device_id={"head": peer(r)},
            device_id_type=MESH,
        )

    def o_copy(c, r):
        to = peer(r)
        return pltpu.make_async_remote_copy(
            src_ref=o_buf.at[c, row_span(to)],
            dst_ref=out_ref.at[:, q_columns(me, c)],
            send_sem=o_send.at[c, r],
            recv_sem=o_recv.at[c, r],
            device_id={"head": to},
            device_id_type=MESH,
        )

    def o_landing(c, r):
        part = out_ref.at[:, q_columns(lax.rem(me + heads - r, heads), c)]
        return pltpu.make_async_remote_copy(
            src_ref=part,
            dst_ref=part,
            send_sem=o_send.at[c, r],
            recv_sem=o_recv.at[c, r],
            device_id={"head": peer(r)},
            device_id_type=MESH,
        )

    own_kv = [
        pltpu.make_async_copy(
            ref.at[:, pl.ds(pl.multiple_of(me * WIDTH, WIDTH), WIDTH)],
            kv_buf.at[n, 0, row_span(me), key_value],
            local_sem.at[n],
        )
        for n, ref in enumerate((k_ref, v_ref))
    ]
    tables = [
        pltpu.make_async_copy(place_ref, place, local_sem.at[2]),
        pltpu.make_async_copy(plan_ref, plan, local_sem.at[3]),
    ]

    def own_q(c):
        return pltpu.make_async_copy(
            q_ref.at[:, q_columns(me, c)], q_buf.at[c, row_span(me)], q_send.at[c, 0]
        )

    def own_o(c):
        return pltpu.make_async_copy(
            o_buf.at[c, row_span(me)], out_ref.at[:, q_columns(me, c)], o_send.at[c, 0]
        )

    barrier = pltpu.get_barrier_semaphore()
    for r in offsets:
        pl.semaphore_signal(barrier, inc=1, device_id={"head": peer(r)}, device_id_type=MESH)
    for origin in origins:
        pl.semaphore_signal(barrier, inc=1, device_id=origin, device_id_type=MESH)
    for copy in own_kv + tables:
        copy.start()
    for c in range(chunks):
        own_q(c).start()
    pl.semaphore_wait(barrier, len(offsets) + len(origins))

    for r in offsets[::-1]:
        kv_copy(0, r).start()
        kv_copy(1, r).start()
    for c in range(EARLY_CHUNKS):
        for r in offsets:
            q_copy(c, r).start()

    for copy in tables:
        copy.wait()
    here = inner * outers + outer
    sources = (
        here,
        lax.rem(inner + inners - 1, inners) * outers + outer,
        lax.rem(inner + inners - 2, inners) * outers + outer,
        inner * outers + lax.rem(outer + outers - 1, outers),
    )
    def starts(block):
        first = block * block_rows
        second = first + run
        out = []
        for spot in (first, second):
            line = place[pl.ds(lax.div(spot, LANES), 1), :]
            lane = lax.broadcasted_iota(jnp.int32, (1, LANES), 1)
            out.append(
                jnp.sum(
                    jnp.where(lane == lax.rem(spot, LANES), line, 0), axis=1, keepdims=True
                )
            )
        return out

    lane = lax.broadcasted_iota(jnp.int32, plan.shape, 1)
    used = jnp.max(jnp.where(lane == here, plan[...], 0), axis=1, keepdims=True)
    q_first, q_second = starts(here)
    q_row = lax.broadcasted_iota(jnp.int32, (block_rows, 1), 0)
    q_place = jnp.where(q_row < run, q_first + q_row, q_second + q_row - run)
    k_row = lax.broadcasted_iota(jnp.int32, (1, block_rows), 1)
    for step, source in enumerate(sources):
        k_first, k_second = starts(source)
        k_place = jnp.where(k_row < run, k_first + k_row, k_second + k_row - run)
        if step:
            k_place = jnp.where(used[step - 1 : step] == 1, k_place, jnp.int32(2**30))
        bias[:, step * block_rows : (step + 1) * block_rows] = jnp.where(
            k_place <= q_place, jnp.float32(0), jnp.float32(MASKED)
        )
    kv_buf[1, :, :, WIDTH:] = jnp.ones((STEPS, block_rows, LANES), kv_buf.dtype)
    logs[...] = jnp.zeros_like(logs)

    for r in pieces:
        for which in range(2):
            if r:
                kv_landing(which, r).wait_recv()
            else:
                own_kv[which].wait()
            next_copies(which, r, lambda copy: copy.start())
    for c in range(EARLY_CHUNKS, chunks):
        for r in offsets:
            q_copy(c, r).start()

    @pl.when(jnp.logical_not(even))
    def _():
        next_landing(0, 0, 0).wait_recv()

    for r in pieces:
        next_landing(side, side, r).wait_recv()
        relay_copy(r).start()
    for r in pieces:
        for which, step in ((1 - side, 1), (0, 2), (1, 2), (side, 1 - side)):
            next_landing(which, step, r).wait_recv()
        if r:
            next_landing(1 - side, 0, r).wait_recv()

    @pl.when(even)
    def _():
        next_landing(1, 0, 0).wait_recv()

    scale = WIDTH**-0.5
    exponent = scale * 1.4426950408889634

    def one_chunk(c, carry):
        own_q(c).wait()
        for r in offsets:
            q_landing(c, r).wait_recv()
        for j in range(CHUNK_HEADS):
            columns = slice(j * WIDTH, (j + 1) * WIDTH)
            for tile in range(0, block_rows, QUERY_TILE):
                span = slice(tile, tile + QUERY_TILE)
                query = q_buf[c, span, columns]
                scores = [
                    lax.dot_general(
                        query,
                        kv_buf[0, step, :, :WIDTH],
                        (((1,), (1,)), ((), ())),
                        preferred_element_type=jnp.float32,
                    )
                    + bias[span, step * block_rows : (step + 1) * block_rows]
                    for step in range(STEPS)
                ]
                top = functools.reduce(jnp.maximum, scores)
                top = jnp.max(top, axis=1, keepdims=True)
                mixed = jnp.zeros((QUERY_TILE, 2 * WIDTH), jnp.float32)
                for step in range(STEPS):
                    weights = jnp.exp2((scores[step] - top) * exponent)
                    mixed += jnp.dot(
                        weights.astype(jnp.bfloat16),
                        kv_buf[1, step],
                        preferred_element_type=jnp.float32,
                    )
                total = mixed[:, WIDTH:]
                o_buf[c, span, columns] = (mixed[:, :WIDTH] / total).astype(o_buf.dtype)
                lane = lax.broadcasted_iota(jnp.int32, (QUERY_TILE, LANES), 1)
                logs[span, :] = jnp.where(
                    lane == c * CHUNK_HEADS + j, top * scale + jnp.log(total), logs[span, :]
                )
        own_o(c).start()
        for r in offsets:
            o_copy(c, r).start()
        return carry

    lax.fori_loop(0, chunks, one_chunk, 0)
    log_ref[...] = jnp.transpose(logs[...])[:GROUP]

    for r in pieces:
        for which in range(2):
            if r:
                kv_copy(which, r).wait_send()
            next_copies(which, r, lambda copy: copy.wait_send())
        relay_copy(r).wait_send()
    for c in range(chunks):
        own_o(c).wait()
        for r in offsets:
            q_copy(c, r).wait_send()
            o_copy(c, r).wait_send()
            o_landing(c, r).wait_recv()


def hand_over(mixed_ref, log_in_ref, out_ref, log_ref, mixed, log, in_sem, out_sem):
    part = mixed_ref.shape[0] // HAND_OVER_PARTS
    spans = [pl.ds(n * part, part) for n in range(HAND_OVER_PARTS)]
    pairs = [(log_in_ref, log, log_ref)] + [
        (mixed_ref.at[span], mixed.at[span], out_ref.at[span]) for span in spans
    ]
    copies = [
        (
            pltpu.make_async_copy(source, stop, in_sem.at[n]),
            pltpu.make_async_copy(stop, end, out_sem.at[n]),
        )
        for n, (source, stop, end) in enumerate(pairs)
    ]
    for load, _ in copies:
        load.start()
    for load, store in copies:
        load.wait()
        store.start()
    for _, store in copies:
        store.wait()


def per_device(queries, keys, values, positions, plan):
    sizes = tuple(lax.axis_size(name) for name in ("head", "inner", "outer"))
    heads = sizes[0]
    rows = queries.shape[0]
    block_rows = rows * heads
    chunks = GROUP // CHUNK_HEADS
    place = positions.reshape(-1, LANES)
    used = plan.T
    anywhere = pl.BlockSpec(memory_space=pl.ANY)
    dma = pltpu.SemaphoreType.DMA
    kind = queries.dtype
    results = pl.pallas_call(
        functools.partial(attention_kernel, sizes),
        out_shape=(
            jax.ShapeDtypeStruct(queries.shape, kind),
            jax.ShapeDtypeStruct((GROUP, block_rows), jnp.float32),
        ),
        in_specs=[anywhere] * 5,
        out_specs=(anywhere, pl.BlockSpec(memory_space=pltpu.VMEM)),
        scratch_shapes=[
            pltpu.VMEM((2, STEPS, block_rows, 2 * WIDTH), kind),
            pltpu.VMEM((chunks, block_rows, CHUNK_HEADS * WIDTH), kind),
            pltpu.VMEM((chunks, block_rows, CHUNK_HEADS * WIDTH), kind),
            pltpu.VMEM((block_rows, STEPS * block_rows), jnp.float32),
            pltpu.VMEM((block_rows, LANES), jnp.float32),
            pltpu.VMEM(place.shape, jnp.int32),
            pltpu.VMEM(used.shape, jnp.int32),
            dma((4,)),
            dma((2, heads)),
            dma((2, heads)),
            dma((2, STEPS - 1, heads)),
            dma((2, STEPS - 1, heads)),
            dma((heads,)),
            dma((chunks, heads)),
            dma((chunks, heads)),
            dma((chunks, heads)),
            dma((chunks, heads)),
        ],
        compiler_params=pltpu.CompilerParams(
            collective_id=0, has_side_effects=True, vmem_limit_bytes=58 * 1024 * 1024
        ),
    )(queries, keys, values, place, used)
    return pl.pallas_call(
        hand_over,
        out_shape=tuple(jax.ShapeDtypeStruct(x.shape, x.dtype) for x in results),
        in_specs=[anywhere] * 2,
        out_specs=(anywhere,) * 2,
        scratch_shapes=[
            *(pltpu.VMEM(x.shape, x.dtype) for x in results),
            dma((HAND_OVER_PARTS + 1,)),
            dma((HAND_OVER_PARTS + 1,)),
        ],
        compiler_params=pltpu.CompilerParams(vmem_limit_bytes=58 * 1024 * 1024),
    )(*results)


def solution(mesh):
    rows = P(("inner", "outer", "head"), None)
    return jax.shard_map(
        per_device,
        mesh=mesh,
        in_specs=(rows, rows, rows, P(), P()),
        out_specs=(rows, P("head", ("inner", "outer"))),
        check_vma=False,
    )
```

```python
import functools

import jax
import jax.numpy as jnp
from jax import lax
from jax.experimental import pallas as pl
from jax.experimental.pallas import tpu as pltpu
from jax.sharding import PartitionSpec as P

WIDTH = 128
GROUP = 8
STEPS = 4
LANES = 128
CHUNK_HEADS = 2
EARLY_CHUNKS = 1
QUERY_TILE = 192
MASKED = -1e30
HAND_OVER_PARTS = 3
MESH = pl.DeviceIdType.MESH


def attention_kernel(
    sizes,
    q_ref,
    k_ref,
    v_ref,
    place_ref,
    plan_ref,
    out_ref,
    log_ref,
    kv_buf,
    q_buf,
    o_buf,
    bias,
    logs,
    place,
    plan,
    local_sem,
    kv_send,
    kv_recv,
    next_send,
    next_recv,
    relay_send,
    relay_recv,
    q_send,
    q_recv,
    o_send,
    o_recv,
):
    heads, inners, outers = sizes
    rows = q_ref.shape[0]
    block_rows = rows * heads
    run = block_rows // 2
    chunks = GROUP // CHUNK_HEADS
    wide = CHUNK_HEADS * WIDTH
    me = lax.axis_index("head")
    inner = lax.axis_index("inner")
    outer = lax.axis_index("outer")
    offsets = sorted(range(1, heads), key=lambda r: -min(r, heads - r))
    pieces = [0] + offsets[::-1]
    side = lax.rem(inner, 2)
    even = side == 0

    def peer(r):
        return lax.rem(me + r, heads)

    def row_span(owner):
        return pl.ds(pl.multiple_of(owner * rows, 16), rows)

    targets = (
        {"inner": lax.rem(inner + 1, inners)},
        {"inner": lax.rem(inner + 2, inners)},
        {"outer": lax.rem(outer + 1, outers)},
    )
    origins = (
        {"inner": lax.rem(inner + inners - 1, inners)},
        {"inner": lax.rem(inner + inners - 2, inners)},
        {"outer": lax.rem(outer + outers - 1, outers)},
    )

    partner = {"inner": inner + 1 - 2 * side}
    key_value = pl.ds(0, WIDTH)

    def kv_copy(which, r):
        ref = (k_ref, v_ref)[which]
        to = peer(r)
        return pltpu.make_async_remote_copy(
            src_ref=ref.at[:, pl.ds(pl.multiple_of(to * WIDTH, WIDTH), WIDTH)],
            dst_ref=kv_buf.at[which, 0, row_span(me), key_value],
            send_sem=kv_send.at[r],
            recv_sem=kv_recv.at[r],
            device_id={"head": to},
            device_id_type=MESH,
        )

    def piece(which, slot, r):
        return kv_buf.at[which, slot, row_span(lax.rem(me + heads - r, heads)), key_value]

    both = slice(None)

    def arrival(part, send_sem, recv_sem):
        return pltpu.make_async_remote_copy(
            src_ref=part,
            dst_ref=part,
            send_sem=send_sem,
            recv_sem=recv_sem,
            device_id=partner,
            device_id_type=MESH,
        )

    def kv_landing(r):
        return arrival(piece(both, 0, r), kv_send.at[r], kv_recv.at[r])

    def next_copy(which, step, r):
        return pltpu.make_async_remote_copy(
            src_ref=piece(which, 0, r),
            dst_ref=piece(which, step + 1, r),
            send_sem=next_send.at[step, r],
            recv_sem=next_recv.at[step, r],
            device_id=targets[step],
            device_id_type=MESH,
        )

    def next_copies(r, act):
        @pl.when(even)
        def _():
            act(next_copy(both, 1, r))
            act(next_copy(both, 0, r))

        @pl.when(jnp.logical_not(even))
        def _():
            act(next_copy(0, 0, r))
            act(next_copy(1, 1, r))

        act(next_copy(both, 2, r))

    def whole_landing(r):
        return arrival(piece(both, 2 - side, r), relay_send.at[r], next_recv.at[1 - side, r])

    def half_landing(r):
        return arrival(piece(side, 1 + side, r), relay_send.at[r], next_recv.at[side, r])

    def outer_landing(r):
        return arrival(piece(both, 3, r), relay_send.at[r], next_recv.at[2, r])

    def relay_copy(r):
        return pltpu.make_async_remote_copy(
            src_ref=piece(side, 1 + side, r),
            dst_ref=piece(side, 2 - side, r),
            send_sem=relay_send.at[r],
            recv_sem=relay_recv.at[r],
            device_id=partner,
            device_id_type=MESH,
        )

    def relay_landing(r):
        return arrival(piece(1 - side, 1 + side, r), relay_send.at[r], relay_recv.at[r])

    def q_columns(owner, c):
        return pl.ds(pl.multiple_of(owner * (GROUP * WIDTH) + c * wide, WIDTH), wide)

    def q_copy(c, r):
        to = peer(r)
        return pltpu.make_async_remote_copy(
            src_ref=q_ref.at[:, q_columns(to, c)],
            dst_ref=q_buf.at[c, row_span(me)],
            send_sem=q_send.at[c, r],
            recv_sem=q_recv.at[c, r],
            device_id={"head": to},
            device_id_type=MESH,
        )

    def q_landing(c, r):
        part = q_buf.at[c, row_span(lax.rem(me + heads - r, heads))]
        return pltpu.make_async_remote_copy(
            src_ref=part,
            dst_ref=part,
            send_sem=q_send.at[c, r],
            recv_sem=q_recv.at[c, r],
            device_id={"head": peer(r)},
            device_id_type=MESH,
        )

    def o_copy(c, r):
        to = peer(r)
        return pltpu.make_async_remote_copy(
            src_ref=o_buf.at[c, row_span(to)],
            dst_ref=out_ref.at[:, q_columns(me, c)],
            send_sem=o_send.at[c, r],
            recv_sem=o_recv.at[c, r],
            device_id={"head": to},
            device_id_type=MESH,
        )

    def o_landing(c, r):
        part = out_ref.at[:, q_columns(lax.rem(me + heads - r, heads), c)]
        return pltpu.make_async_remote_copy(
            src_ref=part,
            dst_ref=part,
            send_sem=o_send.at[c, r],
            recv_sem=o_recv.at[c, r],
            device_id={"head": peer(r)},
            device_id_type=MESH,
        )

    own_kv = [
        pltpu.make_async_copy(
            ref.at[:, pl.ds(pl.multiple_of(me * WIDTH, WIDTH), WIDTH)],
            kv_buf.at[n, 0, row_span(me), key_value],
            local_sem.at[n],
        )
        for n, ref in enumerate((k_ref, v_ref))
    ]
    tables = [
        pltpu.make_async_copy(place_ref, place, local_sem.at[2]),
        pltpu.make_async_copy(plan_ref, plan, local_sem.at[3]),
    ]

    def own_q(c):
        return pltpu.make_async_copy(
            q_ref.at[:, q_columns(me, c)], q_buf.at[c, row_span(me)], q_send.at[c, 0]
        )

    def own_o(c):
        return pltpu.make_async_copy(
            o_buf.at[c, row_span(me)], out_ref.at[:, q_columns(me, c)], o_send.at[c, 0]
        )

    barrier = pltpu.get_barrier_semaphore()
    for r in offsets:
        pl.semaphore_signal(barrier, inc=1, device_id={"head": peer(r)}, device_id_type=MESH)
    for origin in origins:
        pl.semaphore_signal(barrier, inc=1, device_id=origin, device_id_type=MESH)
    for copy in own_kv + tables:
        copy.start()
    for c in range(chunks):
        own_q(c).start()
    pl.semaphore_wait(barrier, len(offsets) + len(origins))

    for r in offsets[::-1]:
        kv_copy(0, r).start()
        kv_copy(1, r).start()

    for copy in own_kv:
        copy.wait()
    next_copies(0, lambda copy: copy.start())
    for c in range(EARLY_CHUNKS):
        for r in offsets:
            q_copy(c, r).start()
    for r in pieces[1:]:
        kv_landing(r).wait_recv()
        next_copies(r, lambda copy: copy.start())
    for c in range(EARLY_CHUNKS, chunks):
        for r in offsets:
            q_copy(c, r).start()

    for copy in tables:
        copy.wait()
    here = inner * outers + outer
    sources = (
        here,
        lax.rem(inner + inners - 1, inners) * outers + outer,
        lax.rem(inner + inners - 2, inners) * outers + outer,
        inner * outers + lax.rem(outer + outers - 1, outers),
    )
    def starts(block):
        first = block * block_rows
        second = first + run
        out = []
        for spot in (first, second):
            line = place[pl.ds(lax.div(spot, LANES), 1), :]
            lane = lax.broadcasted_iota(jnp.int32, (1, LANES), 1)
            out.append(
                jnp.sum(
                    jnp.where(lane == lax.rem(spot, LANES), line, 0), axis=1, keepdims=True
                )
            )
        return out

    lane = lax.broadcasted_iota(jnp.int32, plan.shape, 1)
    used = jnp.max(jnp.where(lane == here, plan[...], 0), axis=1, keepdims=True)
    q_first, q_second = starts(here)
    q_row = lax.broadcasted_iota(jnp.int32, (block_rows, 1), 0)
    q_place = jnp.where(q_row < run, q_first + q_row, q_second + q_row - run)
    k_row = lax.broadcasted_iota(jnp.int32, (1, block_rows), 1)
    for step, source in enumerate(sources):
        k_first, k_second = starts(source)
        k_place = jnp.where(k_row < run, k_first + k_row, k_second + k_row - run)
        if step:
            k_place = jnp.where(used[step - 1 : step] == 1, k_place, jnp.int32(2**30))
        bias[:, step * block_rows : (step + 1) * block_rows] = jnp.where(
            k_place <= q_place, jnp.float32(0), jnp.float32(MASKED)
        )
    kv_buf[1, :, :, WIDTH:] = jnp.ones((STEPS, block_rows, LANES), kv_buf.dtype)
    logs[...] = jnp.zeros_like(logs)

    @pl.when(jnp.logical_not(even))
    def _():
        whole_landing(0).wait_recv()

    for r in pieces:
        half_landing(r).wait_recv()
        relay_copy(r).start()
    for r in pieces:
        outer_landing(r).wait_recv()
        if r:
            whole_landing(r).wait_recv()

    @pl.when(even)
    def _():
        whole_landing(0).wait_recv()

    for r in pieces:
        relay_landing(r).wait_recv()

    scale = WIDTH**-0.5
    exponent = scale * 1.4426950408889634

    def one_chunk(c, carry):
        own_q(c).wait()
        for r in offsets:
            q_landing(c, r).wait_recv()
        for j in range(CHUNK_HEADS):
            columns = slice(j * WIDTH, (j + 1) * WIDTH)
            for tile in range(0, block_rows, QUERY_TILE):
                span = slice(tile, tile + QUERY_TILE)
                query = q_buf[c, span, columns]
                scores = [
                    lax.dot_general(
                        query,
                        kv_buf[0, step, :, :WIDTH],
                        (((1,), (1,)), ((), ())),
                        preferred_element_type=jnp.float32,
                    )
                    + bias[span, step * block_rows : (step + 1) * block_rows]
                    for step in range(STEPS)
                ]
                top = functools.reduce(jnp.maximum, scores)
                top = jnp.max(top, axis=1, keepdims=True)
                mixed = jnp.zeros((QUERY_TILE, 2 * WIDTH), jnp.float32)
                for step in range(STEPS):
                    weights = jnp.exp2((scores[step] - top) * exponent)
                    mixed += jnp.dot(
                        weights.astype(jnp.bfloat16),
                        kv_buf[1, step],
                        preferred_element_type=jnp.float32,
                    )
                total = mixed[:, WIDTH:]
                o_buf[c, span, columns] = (mixed[:, :WIDTH] / total).astype(o_buf.dtype)
                lane = lax.broadcasted_iota(jnp.int32, (QUERY_TILE, LANES), 1)
                logs[span, :] = jnp.where(
                    lane == c * CHUNK_HEADS + j, top * scale + jnp.log(total), logs[span, :]
                )
        own_o(c).start()
        for r in offsets:
            o_copy(c, r).start()
        return carry

    lax.fori_loop(0, chunks, one_chunk, 0)
    log_ref[...] = jnp.transpose(logs[...])[:GROUP]

    for r in pieces:
        if r:
            kv_landing(r).wait_send()
        next_copies(r, lambda copy: copy.wait_send())
        relay_copy(r).wait_send()
    for c in range(chunks):
        own_o(c).wait()
        for r in offsets:
            q_copy(c, r).wait_send()
            o_copy(c, r).wait_send()
            o_landing(c, r).wait_recv()


def hand_over(mixed_ref, log_in_ref, out_ref, log_ref, sem):
    part = mixed_ref.shape[0] // HAND_OVER_PARTS
    copies = [pltpu.make_async_copy(log_in_ref, log_ref, sem.at[HAND_OVER_PARTS])]
    for n in range(HAND_OVER_PARTS):
        span = pl.ds(n * part, part)
        copies.append(pltpu.make_async_copy(mixed_ref.at[span], out_ref.at[span], sem.at[n]))
    for copy in copies:
        copy.start()
    for copy in copies:
        copy.wait()


def per_device(queries, keys, values, positions, plan):
    sizes = tuple(lax.axis_size(name) for name in ("head", "inner", "outer"))
    heads = sizes[0]
    rows = queries.shape[0]
    block_rows = rows * heads
    chunks = GROUP // CHUNK_HEADS
    place = positions.reshape(-1, LANES)
    used = plan.T
    anywhere = pl.BlockSpec(memory_space=pl.ANY)
    dma = pltpu.SemaphoreType.DMA
    kind = queries.dtype
    queries, keys, values, place, used = (
        pltpu.with_memory_space_constraint(x, pltpu.HBM)
        for x in (queries, keys, values, place, used)
    )
    results = pl.pallas_call(
        functools.partial(attention_kernel, sizes),
        out_shape=(
            jax.ShapeDtypeStruct(queries.shape, kind),
            jax.ShapeDtypeStruct((GROUP, block_rows), jnp.float32),
        ),
        in_specs=[anywhere] * 5,
        out_specs=(anywhere, pl.BlockSpec(memory_space=pltpu.VMEM)),
        scratch_shapes=[
            pltpu.VMEM((2, STEPS, block_rows, 2 * WIDTH), kind),
            pltpu.VMEM((chunks, block_rows, CHUNK_HEADS * WIDTH), kind),
            pltpu.VMEM((chunks, block_rows, CHUNK_HEADS * WIDTH), kind),
            pltpu.VMEM((block_rows, STEPS * block_rows), jnp.float32),
            pltpu.VMEM((block_rows, LANES), jnp.float32),
            pltpu.VMEM(place.shape, jnp.int32),
            pltpu.VMEM(used.shape, jnp.int32),
            dma((4,)),
            dma((heads,)),
            dma((heads,)),
            dma((STEPS - 1, heads)),
            dma((STEPS - 1, heads)),
            dma((heads,)),
            dma((heads,)),
            dma((chunks, heads)),
            dma((chunks, heads)),
            dma((chunks, heads)),
            dma((chunks, heads)),
        ],
        compiler_params=pltpu.CompilerParams(
            collective_id=0, has_side_effects=True, vmem_limit_bytes=30 * 1024 * 1024
        ),
    )(queries, keys, values, place, used)
    return pl.pallas_call(
        hand_over,
        out_shape=tuple(jax.ShapeDtypeStruct(x.shape, x.dtype) for x in results),
        in_specs=[anywhere] * 2,
        out_specs=(anywhere,) * 2,
        scratch_shapes=[
            dma((HAND_OVER_PARTS + 1,)),
        ],
        compiler_params=pltpu.CompilerParams(vmem_limit_bytes=30 * 1024 * 1024),
    )(*results)


def solution(mesh):
    rows = P(("inner", "outer", "head"), None)
    return jax.shard_map(
        per_device,
        mesh=mesh,
        in_specs=(rows, rows, rows, P(), P()),
        out_specs=(rows, P("head", ("inner", "outer"))),
        check_vma=False,
    )
```

```python
import functools

import jax
import jax.numpy as jnp
from jax import lax
from jax.experimental import pallas as pl
from jax.experimental.pallas import tpu as pltpu
from jax.sharding import PartitionSpec as P

WIDTH = 128
GROUP = 8
STEPS = 4
LANES = 128
CHUNK_HEADS = 2
EARLY_CHUNKS = 1
QUERY_TILE = 192
MASKED = -1e30
NEAR = (0, 3)
FAR = (1, 2)
HAND_OVER_PARTS = 3
MESH = pl.DeviceIdType.MESH


def attention_kernel(
    sizes,
    q_ref,
    k_ref,
    v_ref,
    place_ref,
    plan_ref,
    out_ref,
    log_ref,
    kv_buf,
    q_buf,
    o_buf,
    bias,
    logs,
    first_top,
    first_mixed,
    place,
    plan,
    local_sem,
    kv_send,
    kv_recv,
    next_send,
    next_recv,
    relay_send,
    relay_recv,
    block_sem,
    go,
    q_send,
    q_recv,
    o_send,
    o_recv,
    first_send,
    first_recv,
):
    heads, inners, outers = sizes
    rows = q_ref.shape[0]
    block_rows = rows * heads
    run = block_rows // 2
    chunks = GROUP // CHUNK_HEADS
    wide = CHUNK_HEADS * WIDTH
    me = lax.axis_index("head")
    inner = lax.axis_index("inner")
    outer = lax.axis_index("outer")
    offsets = sorted(range(1, heads), key=lambda r: -min(r, heads - r))
    pieces = [0] + offsets[::-1]
    side = lax.rem(inner, 2)
    even = side == 0

    def peer(r):
        return lax.rem(me + r, heads)

    def row_span(owner):
        return pl.ds(pl.multiple_of(owner * rows, 16), rows)

    targets = (
        {"inner": lax.rem(inner + 1, inners)},
        {"inner": lax.rem(inner + 2, inners)},
        {"outer": lax.rem(outer + 1, outers)},
    )
    origins = (
        {"inner": lax.rem(inner + inners - 1, inners)},
        {"inner": lax.rem(inner + inners - 2, inners)},
        {"outer": lax.rem(outer + outers - 1, outers)},
    )

    partner = {"inner": inner + 1 - 2 * side}
    key_value = pl.ds(0, WIDTH)

    def kv_copy(which, r):
        ref = (k_ref, v_ref)[which]
        to = peer(r)
        return pltpu.make_async_remote_copy(
            src_ref=ref.at[:, pl.ds(pl.multiple_of(to * WIDTH, WIDTH), WIDTH)],
            dst_ref=kv_buf.at[which, 0, row_span(me), key_value],
            send_sem=kv_send.at[r],
            recv_sem=kv_recv.at[r],
            device_id={"head": to},
            device_id_type=MESH,
        )

    def piece(which, slot, r):
        return kv_buf.at[which, slot, row_span(lax.rem(me + heads - r, heads)), key_value]

    both = slice(None)

    def arrival(part, send_sem, recv_sem):
        return pltpu.make_async_remote_copy(
            src_ref=part,
            dst_ref=part,
            send_sem=send_sem,
            recv_sem=recv_sem,
            device_id=partner,
            device_id_type=MESH,
        )

    def kv_landing(r):
        return arrival(piece(both, 0, r), kv_send.at[r], kv_recv.at[r])

    def next_copy(which, step, r):
        return pltpu.make_async_remote_copy(
            src_ref=piece(which, 0, r),
            dst_ref=piece(which, step + 1, r),
            send_sem=next_send.at[step, r],
            recv_sem=next_recv.at[step, r],
            device_id=targets[step],
            device_id_type=MESH,
        )

    def next_copies(r, act):
        @pl.when(even)
        def _():
            act(next_copy(both, 0, r))

        @pl.when(jnp.logical_not(even))
        def _():
            act(next_copy(both, 1, r))

        act(next_copy(both, 2, r))

    def block_copy():
        return pltpu.make_async_remote_copy(
            src_ref=kv_buf.at[:, 0, :, key_value],
            dst_ref=kv_buf.at[:, 2, :, key_value],
            send_sem=block_sem.at[0],
            recv_sem=block_sem.at[1],
            device_id=targets[1],
            device_id_type=MESH,
        )

    def near_landing(r):
        return arrival(piece(both, 1, r), relay_send.at[r], next_recv.at[0, r])

    def far_landing(r):
        return arrival(piece(both, 2, r), relay_send.at[r], next_recv.at[1, r])

    def outer_landing(r):
        return arrival(piece(both, 3, r), relay_send.at[r], next_recv.at[2, r])

    def relay_copy(r):
        return pltpu.make_async_remote_copy(
            src_ref=piece(both, 2, r),
            dst_ref=piece(both, 1, r),
            send_sem=relay_send.at[r],
            recv_sem=relay_recv.at[r],
            device_id=partner,
            device_id_type=MESH,
        )

    def relay_landing(r):
        return arrival(piece(both, 1, r), relay_send.at[r], relay_recv.at[r])

    def q_columns(owner, c):
        return pl.ds(pl.multiple_of(owner * (GROUP * WIDTH) + c * wide, WIDTH), wide)

    def q_copy(c, r):
        to = peer(r)
        return pltpu.make_async_remote_copy(
            src_ref=q_ref.at[:, q_columns(to, c)],
            dst_ref=q_buf.at[c, row_span(me)],
            send_sem=q_send.at[c, r],
            recv_sem=q_recv.at[c, r],
            device_id={"head": to},
            device_id_type=MESH,
        )

    def q_landing(c, r):
        part = q_buf.at[c, row_span(lax.rem(me + heads - r, heads))]
        return pltpu.make_async_remote_copy(
            src_ref=part,
            dst_ref=part,
            send_sem=q_send.at[c, r],
            recv_sem=q_recv.at[c, r],
            device_id={"head": peer(r)},
            device_id_type=MESH,
        )

    def o_copy(c, r):
        to = peer(r)
        return pltpu.make_async_remote_copy(
            src_ref=o_buf.at[c, row_span(to)],
            dst_ref=out_ref.at[:, q_columns(me, c)],
            send_sem=o_send.at[c, r],
            recv_sem=o_recv.at[c, r],
            device_id={"head": to},
            device_id_type=MESH,
        )

    def o_landing(c, r):
        part = out_ref.at[:, q_columns(lax.rem(me + heads - r, heads), c)]
        return pltpu.make_async_remote_copy(
            src_ref=part,
            dst_ref=part,
            send_sem=o_send.at[c, r],
            recv_sem=o_recv.at[c, r],
            device_id={"head": peer(r)},
            device_id_type=MESH,
        )

    def head_columns(owner, j):
        return pl.ds(pl.multiple_of((owner * GROUP + j) * WIDTH, WIDTH), WIDTH)

    def first_copy(j, r):
        to = peer(r)
        return pltpu.make_async_remote_copy(
            src_ref=o_buf.at[0, row_span(to), pl.ds(j * WIDTH, WIDTH)],
            dst_ref=out_ref.at[:, head_columns(me, j)],
            send_sem=first_send.at[j, r],
            recv_sem=first_recv.at[j, r],
            device_id={"head": to},
            device_id_type=MESH,
        )

    def first_landing(j, r):
        part = out_ref.at[:, head_columns(lax.rem(me + heads - r, heads), j)]
        return arrival(part, first_send.at[j, r], first_recv.at[j, r])

    def own_first(j):
        return pltpu.make_async_copy(
            o_buf.at[0, row_span(me), pl.ds(j * WIDTH, WIDTH)],
            out_ref.at[:, head_columns(me, j)],
            first_send.at[j, 0],
        )

    own_kv = [
        pltpu.make_async_copy(
            ref.at[:, pl.ds(pl.multiple_of(me * WIDTH, WIDTH), WIDTH)],
            kv_buf.at[n, 0, row_span(me), key_value],
            local_sem.at[n],
        )
        for n, ref in enumerate((k_ref, v_ref))
    ]
    tables = [
        pltpu.make_async_copy(place_ref, place, local_sem.at[2]),
        pltpu.make_async_copy(plan_ref, plan, local_sem.at[3]),
    ]

    def own_q(c):
        return pltpu.make_async_copy(
            q_ref.at[:, q_columns(me, c)], q_buf.at[c, row_span(me)], q_send.at[c, 0]
        )

    def own_o(c):
        return pltpu.make_async_copy(
            o_buf.at[c, row_span(me)], out_ref.at[:, q_columns(me, c)], o_send.at[c, 0]
        )

    barrier = pltpu.get_barrier_semaphore()
    for r in offsets:
        pl.semaphore_signal(barrier, inc=1, device_id={"head": peer(r)}, device_id_type=MESH)
    for origin in origins:
        pl.semaphore_signal(barrier, inc=1, device_id=origin, device_id_type=MESH)
    for copy in own_kv:
        copy.start()
    pl.semaphore_wait(barrier, len(offsets) + len(origins))

    for r in offsets[::-1]:
        kv_copy(0, r).start()
        kv_copy(1, r).start()

    for copy in own_kv:
        copy.wait()
    for copy in tables:
        copy.start()
    next_copies(0, lambda copy: copy.start())
    for c in range(EARLY_CHUNKS):
        for r in offsets:
            q_copy(c, r).start()
    for r in pieces[1:]:
        kv_landing(r).wait_recv()
        next_copies(r, lambda copy: copy.start())
    for c in range(EARLY_CHUNKS, chunks):
        for r in offsets:
            q_copy(c, r).start()

    for c in range(chunks):
        own_q(c).start()
    for copy in tables:
        copy.wait()
    here = inner * outers + outer
    sources = (
        here,
        lax.rem(inner + inners - 1, inners) * outers + outer,
        lax.rem(inner + inners - 2, inners) * outers + outer,
        inner * outers + lax.rem(outer + outers - 1, outers),
    )
    def starts(block):
        first = block * block_rows
        second = first + run
        out = []
        for spot in (first, second):
            line = place[pl.ds(lax.div(spot, LANES), 1), :]
            lane = lax.broadcasted_iota(jnp.int32, (1, LANES), 1)
            out.append(
                jnp.sum(
                    jnp.where(lane == lax.rem(spot, LANES), line, 0), axis=1, keepdims=True
                )
            )
        return out

    lane = lax.broadcasted_iota(jnp.int32, plan.shape, 1)
    used = jnp.max(jnp.where(lane == here, plan[...], 0), axis=1, keepdims=True)
    q_first, q_second = starts(here)
    q_row = lax.broadcasted_iota(jnp.int32, (block_rows, 1), 0)
    q_place = jnp.where(q_row < run, q_first + q_row, q_second + q_row - run)
    k_row = lax.broadcasted_iota(jnp.int32, (1, block_rows), 1)
    for step, source in enumerate(sources):
        k_first, k_second = starts(source)
        k_place = jnp.where(k_row < run, k_first + k_row, k_second + k_row - run)
        if step:
            k_place = jnp.where(used[step - 1 : step] == 1, k_place, jnp.int32(2**30))
        bias[:, step * block_rows : (step + 1) * block_rows] = jnp.where(
            k_place <= q_place, jnp.float32(0), jnp.float32(MASKED)
        )
    kv_buf[1, :, :, WIDTH:] = jnp.ones((STEPS, block_rows, LANES), kv_buf.dtype)
    logs[...] = jnp.zeros_like(logs)

    scale = WIDTH**-0.5
    exponent = scale * 1.4426950408889634

    def one_head(c, j, finish):
        for tile in range(0, block_rows, QUERY_TILE):
            span = slice(tile, tile + QUERY_TILE)
            query = q_buf[c, span, j * WIDTH : (j + 1) * WIDTH]
            finish(c, j, span, query)

    def fold(query, span, steps, prior=None):
        scores = [
            lax.dot_general(
                query,
                kv_buf[0, step, :, :WIDTH],
                (((1,), (1,)), ((), ())),
                preferred_element_type=jnp.float32,
            )
            + bias[span, step * block_rows : (step + 1) * block_rows]
            for step in steps
        ]
        top = functools.reduce(jnp.maximum, scores)
        top = jnp.max(top, axis=1, keepdims=True)
        mixed = jnp.zeros((QUERY_TILE, 2 * WIDTH), jnp.float32)
        if prior is not None:
            before, mixed = prior
            top = jnp.maximum(top, before)
            mixed = mixed * jnp.exp2((before - top) * exponent)
        for score, step in zip(scores, steps):
            weights = jnp.exp2((score - top) * exponent)
            mixed += jnp.dot(
                weights.astype(jnp.bfloat16),
                kv_buf[1, step],
                preferred_element_type=jnp.float32,
            )
        return top, mixed

    def write(c, j, span, top, mixed):
        total = mixed[:, WIDTH:]
        o_buf[c, span, j * WIDTH : (j + 1) * WIDTH] = (mixed[:, :WIDTH] / total).astype(
            o_buf.dtype
        )
        lane = lax.broadcasted_iota(jnp.int32, (QUERY_TILE, LANES), 1)
        logs[span, :] = jnp.where(
            lane == c * CHUNK_HEADS + j, top * scale + jnp.log(total), logs[span, :]
        )

    def near_part(c, j, span, query):
        top, mixed = fold(query, span, NEAR)
        first_top[span, :] = jnp.broadcast_to(top, (QUERY_TILE, LANES))
        first_mixed[span, :] = mixed

    def far_part(c, j, span, query):
        prior = (first_top[span, :1], first_mixed[span, :])
        write(c, j, span, *fold(query, span, FAR, prior))

    def whole(c, j, span, query):
        write(c, j, span, *fold(query, span, range(STEPS)))

    def take_queries(c):
        own_q(c).wait()
        for r in offsets:
            q_landing(c, r).wait_recv()

    @pl.when(jnp.logical_not(even))
    def _():
        for r in pieces:
            next_copy(both, 1, r).wait_send()
        near_landing(0).wait_recv()
        pl.semaphore_signal(go, inc=1, device_id=partner, device_id_type=MESH)

    @pl.when(even)
    def _():
        pl.semaphore_wait(go, 1)
        block_copy().start()

    for r in pieces:
        outer_landing(r).wait_recv()
    take_queries(0)
    one_head(0, 0, near_part)

    @pl.when(jnp.logical_not(even))
    def _():
        for r in pieces[1:]:
            near_landing(r).wait_recv()
        for r in pieces:
            far_landing(r).wait_recv()
            relay_copy(r).start()

    @pl.when(even)
    def _():
        for r in pieces:
            relay_landing(r).wait_recv()
        block_copy().wait_recv()

    for j in range(CHUNK_HEADS):
        one_head(0, j, whole if j else far_part)
        own_first(j).start()
        for r in offsets:
            first_copy(j, r).start()

    def one_chunk(c, carry):
        take_queries(c)
        for j in range(CHUNK_HEADS):
            one_head(c, j, whole)
        own_o(c).start()
        for r in offsets:
            o_copy(c, r).start()
        return carry

    lax.fori_loop(1, chunks, one_chunk, 0)
    log_ref[...] = jnp.transpose(logs[...])[:GROUP]

    for r in pieces:
        if r:
            kv_landing(r).wait_send()
        next_copy(both, 2, r).wait_send()

    @pl.when(even)
    def _():
        for r in pieces:
            next_copy(both, 0, r).wait_send()
        block_copy().wait_send()

    @pl.when(jnp.logical_not(even))
    def _():
        for r in pieces:
            relay_copy(r).wait_send()

    for j in range(CHUNK_HEADS):
        own_first(j).wait()
        for r in offsets:
            first_copy(j, r).wait_send()
            first_landing(j, r).wait_recv()
    for r in offsets:
        q_copy(0, r).wait_send()
    for c in range(1, chunks):
        own_o(c).wait()
        for r in offsets:
            q_copy(c, r).wait_send()
            o_copy(c, r).wait_send()
            o_landing(c, r).wait_recv()


def hand_over(mixed_ref, log_in_ref, out_ref, log_ref, sem):
    part = mixed_ref.shape[0] // HAND_OVER_PARTS
    copies = [pltpu.make_async_copy(log_in_ref, log_ref, sem.at[HAND_OVER_PARTS])]
    for n in range(HAND_OVER_PARTS):
        span = pl.ds(n * part, part)
        copies.append(pltpu.make_async_copy(mixed_ref.at[span], out_ref.at[span], sem.at[n]))
    for copy in copies:
        copy.start()
    for copy in copies:
        copy.wait()


def per_device(queries, keys, values, positions, plan):
    sizes = tuple(lax.axis_size(name) for name in ("head", "inner", "outer"))
    heads = sizes[0]
    rows = queries.shape[0]
    block_rows = rows * heads
    chunks = GROUP // CHUNK_HEADS
    place = positions.reshape(-1, LANES)
    used = plan.T
    anywhere = pl.BlockSpec(memory_space=pl.ANY)
    dma = pltpu.SemaphoreType.DMA
    kind = queries.dtype
    queries, keys, values, place, used = (
        pltpu.with_memory_space_constraint(x, pltpu.HBM)
        for x in (queries, keys, values, place, used)
    )
    results = pl.pallas_call(
        functools.partial(attention_kernel, sizes),
        out_shape=(
            jax.ShapeDtypeStruct(queries.shape, kind),
            jax.ShapeDtypeStruct((GROUP, block_rows), jnp.float32),
        ),
        in_specs=[anywhere] * 5,
        out_specs=(anywhere, pl.BlockSpec(memory_space=pltpu.VMEM)),
        scratch_shapes=[
            pltpu.VMEM((2, STEPS, block_rows, 2 * WIDTH), kind),
            pltpu.VMEM((chunks, block_rows, CHUNK_HEADS * WIDTH), kind),
            pltpu.VMEM((chunks, block_rows, CHUNK_HEADS * WIDTH), kind),
            pltpu.VMEM((block_rows, STEPS * block_rows), jnp.float32),
            pltpu.VMEM((block_rows, LANES), jnp.float32),
            pltpu.VMEM((block_rows, LANES), jnp.float32),
            pltpu.VMEM((block_rows, 2 * WIDTH), jnp.float32),
            pltpu.VMEM(place.shape, jnp.int32),
            pltpu.VMEM(used.shape, jnp.int32),
            dma((4,)),
            dma((heads,)),
            dma((heads,)),
            dma((STEPS - 1, heads)),
            dma((STEPS - 1, heads)),
            dma((heads,)),
            dma((heads,)),
            dma((2,)),
            pltpu.SemaphoreType.REGULAR,
            dma((chunks, heads)),
            dma((chunks, heads)),
            dma((chunks, heads)),
            dma((chunks, heads)),
            dma((CHUNK_HEADS, heads)),
            dma((CHUNK_HEADS, heads)),
        ],
        compiler_params=pltpu.CompilerParams(
            collective_id=0, has_side_effects=True, vmem_limit_bytes=30 * 1024 * 1024
        ),
    )(queries, keys, values, place, used)
    return pl.pallas_call(
        hand_over,
        out_shape=tuple(jax.ShapeDtypeStruct(x.shape, x.dtype) for x in results),
        in_specs=[anywhere] * 2,
        out_specs=(anywhere,) * 2,
        scratch_shapes=[
            dma((HAND_OVER_PARTS + 1,)),
        ],
        compiler_params=pltpu.CompilerParams(vmem_limit_bytes=30 * 1024 * 1024),
    )(*results)


def solution(mesh):
    rows = P(("inner", "outer", "head"), None)
    return jax.shard_map(
        per_device,
        mesh=mesh,
        in_specs=(rows, rows, rows, P(), P()),
        out_specs=(rows, P("head", ("inner", "outer"))),
        check_vma=False,
    )
```

```python
import functools

import jax
import jax.numpy as jnp
from jax import lax
from jax.experimental import pallas as pl
from jax.experimental.pallas import tpu as pltpu
from jax.sharding import PartitionSpec as P

WIDTH = 128
GROUP = 8
STEPS = 4
LANES = 128
CHUNK_HEADS = 2
EARLY_CHUNKS = 1
QUERY_TILE = 192
MASKED = -1e30
NEAR = (0, 3)
FAR = (1, 2)
HAND_OVER_PARTS = 3
MESH = pl.DeviceIdType.MESH


def attention_kernel(
    sizes,
    q_ref,
    k_ref,
    v_ref,
    place_ref,
    plan_ref,
    out_ref,
    log_ref,
    kv_buf,
    q_buf,
    o_buf,
    bias,
    logs,
    first_top,
    first_mixed,
    place,
    plan,
    local_sem,
    kv_send,
    kv_recv,
    next_send,
    next_recv,
    relay_send,
    relay_recv,
    block_sem,
    go,
    ready,
    q_send,
    q_recv,
    o_send,
    o_recv,
    first_send,
    first_recv,
):
    heads, inners, outers = sizes
    rows = q_ref.shape[0]
    block_rows = rows * heads
    run = block_rows // 2
    chunks = GROUP // CHUNK_HEADS
    wide = CHUNK_HEADS * WIDTH
    me = lax.axis_index("head")
    inner = lax.axis_index("inner")
    outer = lax.axis_index("outer")
    offsets = sorted(range(1, heads), key=lambda r: -min(r, heads - r))
    pieces = [0] + offsets[::-1]
    side = lax.rem(inner, 2)
    even = side == 0
    first_cycle = inner < 2

    def peer(r):
        return lax.rem(me + r, heads)

    def row_span(owner):
        return pl.ds(pl.multiple_of(owner * rows, 16), rows)

    targets = (
        {"inner": lax.rem(inner + 1, inners)},
        {"inner": lax.rem(inner + 2, inners)},
        {"outer": lax.rem(outer + 1, outers)},
    )
    outer_origin = {"outer": lax.rem(outer + outers - 1, outers)}
    inner_origin = {"inner": lax.rem(inner + inners - 2, inners)}
    wraps = inner >= inners - 2
    wrapped = inner < 2
    second = jnp.logical_and(wraps, even)
    ahead = jnp.logical_not(jnp.logical_or(wraps, even))
    partner = {"inner": inner + 1 - 2 * side}
    key_value = pl.ds(0, WIDTH)

    def kv_copy(which, r):
        ref = (k_ref, v_ref)[which]
        to = peer(r)
        return pltpu.make_async_remote_copy(
            src_ref=ref.at[:, pl.ds(pl.multiple_of(to * WIDTH, WIDTH), WIDTH)],
            dst_ref=kv_buf.at[which, 0, row_span(me), key_value],
            send_sem=kv_send.at[r],
            recv_sem=kv_recv.at[r],
            device_id={"head": to},
            device_id_type=MESH,
        )

    def piece(which, slot, r):
        return kv_buf.at[which, slot, row_span(lax.rem(me + heads - r, heads)), key_value]

    both = slice(None)

    def arrival(part, send_sem, recv_sem):
        return pltpu.make_async_remote_copy(
            src_ref=part,
            dst_ref=part,
            send_sem=send_sem,
            recv_sem=recv_sem,
            device_id=partner,
            device_id_type=MESH,
        )

    def kv_landing(r):
        return arrival(piece(both, 0, r), kv_send.at[r], kv_recv.at[r])

    def next_copy(which, step, r):
        return pltpu.make_async_remote_copy(
            src_ref=piece(which, 0, r),
            dst_ref=piece(which, step + 1, r),
            send_sem=next_send.at[step, r],
            recv_sem=next_recv.at[step, r],
            device_id=targets[step],
            device_id_type=MESH,
        )

    def next_copies(r, act):
        @pl.when(even)
        def _():
            act(next_copy(both, 0, r))

        @pl.when(jnp.logical_not(even))
        def _():
            act(next_copy(both, 1, r))

        act(next_copy(both, 2, r))

    def block_copy():
        return pltpu.make_async_remote_copy(
            src_ref=kv_buf.at[:, 0, :, key_value],
            dst_ref=kv_buf.at[:, 2, :, key_value],
            send_sem=block_sem.at[0],
            recv_sem=block_sem.at[1],
            device_id=targets[1],
            device_id_type=MESH,
        )

    def near_landing(r):
        return arrival(piece(both, 1, r), relay_send.at[r], next_recv.at[0, r])

    def far_landing(r):
        return arrival(piece(both, 2, r), relay_send.at[r], next_recv.at[1, r])

    def outer_landing(r):
        return arrival(piece(both, 3, r), relay_send.at[r], next_recv.at[2, r])

    def relay_copy(r):
        return pltpu.make_async_remote_copy(
            src_ref=piece(both, 2, r),
            dst_ref=piece(both, 1, r),
            send_sem=relay_send.at[r],
            recv_sem=relay_recv.at[r],
            device_id=partner,
            device_id_type=MESH,
        )

    def relay_landing(r):
        return arrival(piece(both, 1, r), relay_send.at[r], relay_recv.at[r])

    def q_columns(owner, c):
        return pl.ds(pl.multiple_of(owner * (GROUP * WIDTH) + c * wide, WIDTH), wide)

    def q_copy(c, r):
        to = peer(r)
        return pltpu.make_async_remote_copy(
            src_ref=q_ref.at[:, q_columns(to, c)],
            dst_ref=q_buf.at[c, row_span(me)],
            send_sem=q_send.at[c, r],
            recv_sem=q_recv.at[c, r],
            device_id={"head": to},
            device_id_type=MESH,
        )

    def q_landing(c, r):
        part = q_buf.at[c, row_span(lax.rem(me + heads - r, heads))]
        return pltpu.make_async_remote_copy(
            src_ref=part,
            dst_ref=part,
            send_sem=q_send.at[c, r],
            recv_sem=q_recv.at[c, r],
            device_id={"head": peer(r)},
            device_id_type=MESH,
        )

    def o_copy(c, r):
        to = peer(r)
        return pltpu.make_async_remote_copy(
            src_ref=o_buf.at[c, row_span(to)],
            dst_ref=out_ref.at[:, q_columns(me, c)],
            send_sem=o_send.at[c, r],
            recv_sem=o_recv.at[c, r],
            device_id={"head": to},
            device_id_type=MESH,
        )

    def o_landing(c, r):
        part = out_ref.at[:, q_columns(lax.rem(me + heads - r, heads), c)]
        return pltpu.make_async_remote_copy(
            src_ref=part,
            dst_ref=part,
            send_sem=o_send.at[c, r],
            recv_sem=o_recv.at[c, r],
            device_id={"head": peer(r)},
            device_id_type=MESH,
        )

    def head_columns(owner, j):
        return pl.ds(pl.multiple_of((owner * GROUP + j) * WIDTH, WIDTH), WIDTH)

    def first_copy(j, r):
        to = peer(r)
        return pltpu.make_async_remote_copy(
            src_ref=o_buf.at[0, row_span(to), pl.ds(j * WIDTH, WIDTH)],
            dst_ref=out_ref.at[:, head_columns(me, j)],
            send_sem=first_send.at[j, r],
            recv_sem=first_recv.at[j, r],
            device_id={"head": to},
            device_id_type=MESH,
        )

    def first_landing(j, r):
        part = out_ref.at[:, head_columns(lax.rem(me + heads - r, heads), j)]
        return arrival(part, first_send.at[j, r], first_recv.at[j, r])

    def own_first(j):
        return pltpu.make_async_copy(
            o_buf.at[0, row_span(me), pl.ds(j * WIDTH, WIDTH)],
            out_ref.at[:, head_columns(me, j)],
            first_send.at[j, 0],
        )

    own_kv = [
        pltpu.make_async_copy(
            ref.at[:, pl.ds(pl.multiple_of(me * WIDTH, WIDTH), WIDTH)],
            kv_buf.at[n, 0, row_span(me), key_value],
            local_sem.at[n],
        )
        for n, ref in enumerate((k_ref, v_ref))
    ]
    tables = [
        pltpu.make_async_copy(place_ref, place, local_sem.at[2]),
        pltpu.make_async_copy(plan_ref, plan, local_sem.at[3]),
    ]

    def own_q(c):
        return pltpu.make_async_copy(
            q_ref.at[:, q_columns(me, c)], q_buf.at[c, row_span(me)], q_send.at[c, 0]
        )

    def own_o(c):
        return pltpu.make_async_copy(
            o_buf.at[c, row_span(me)], out_ref.at[:, q_columns(me, c)], o_send.at[c, 0]
        )

    barrier = pltpu.get_barrier_semaphore()
    for r in offsets:
        pl.semaphore_signal(barrier, inc=1, device_id={"head": peer(r)}, device_id_type=MESH)
    pl.semaphore_signal(barrier, inc=1, device_id=outer_origin, device_id_type=MESH)

    @pl.when(jnp.logical_not(even))
    def _():
        pl.semaphore_signal(barrier, inc=1, device_id=partner, device_id_type=MESH)

    @pl.when(wrapped)
    def _():
        pl.semaphore_signal(barrier, inc=1, device_id=inner_origin, device_id_type=MESH)

    @pl.when(jnp.logical_not(wraps))
    def _():
        pl.semaphore_signal(barrier, inc=1, device_id=targets[1], device_id_type=MESH)

    for copy in own_kv + tables:
        copy.start()
    in_last = lax.div(inner, inners - 2)
    in_first = lax.div(inners - 1 - inner, inners - 2)
    pl.semaphore_wait(barrier, len(offsets) + 1 + (1 - side) + in_last + (1 - in_first))

    @pl.when(jnp.logical_not(wrapped))
    def _():
        pl.semaphore_signal(ready, inc=1, device_id=inner_origin, device_id_type=MESH)


    def make_mask():
        for copy in tables:
            copy.wait()
        here = inner * outers + outer
        sources = (
            here,
            lax.rem(inner + inners - 1, inners) * outers + outer,
            lax.rem(inner + inners - 2, inners) * outers + outer,
            inner * outers + lax.rem(outer + outers - 1, outers),
        )
        def starts(block):
            first = block * block_rows
            second = first + run
            out = []
            for spot in (first, second):
                line = place[pl.ds(lax.div(spot, LANES), 1), :]
                lane = lax.broadcasted_iota(jnp.int32, (1, LANES), 1)
                out.append(
                    jnp.sum(
                        jnp.where(lane == lax.rem(spot, LANES), line, 0), axis=1, keepdims=True
                    )
                )
            return out

        lane = lax.broadcasted_iota(jnp.int32, plan.shape, 1)
        used = jnp.max(jnp.where(lane == here, plan[...], 0), axis=1, keepdims=True)
        q_first, q_second = starts(here)
        q_row = lax.broadcasted_iota(jnp.int32, (block_rows, 1), 0)
        q_place = jnp.where(q_row < run, q_first + q_row, q_second + q_row - run)
        k_row = lax.broadcasted_iota(jnp.int32, (1, block_rows), 1)
        for step, source in enumerate(sources):
            k_first, k_second = starts(source)
            k_place = jnp.where(k_row < run, k_first + k_row, k_second + k_row - run)
            if step:
                k_place = jnp.where(used[step - 1 : step] == 1, k_place, jnp.int32(2**30))
            bias[:, step * block_rows : (step + 1) * block_rows] = jnp.where(
                k_place <= q_place, jnp.float32(0), jnp.float32(MASKED)
            )

    @pl.when(second)
    def _():
        make_mask()

    for r in offsets[::-1]:
        kv_copy(0, r).start()
        kv_copy(1, r).start()

    for copy in own_kv:
        copy.wait()
    for c in range(EARLY_CHUNKS):
        for r in offsets:
            q_copy(c, r).start()

    @pl.when(ahead)
    def _():
        for c in range(EARLY_CHUNKS, chunks):
            for r in offsets:
                q_copy(c, r).start()

    @pl.when(ahead)
    def _():
        pl.semaphore_wait(ready, 1)

    next_copies(0, lambda copy: copy.start())
    for r in pieces[1:]:
        kv_landing(r).wait_recv()
        next_copies(r, lambda copy: copy.start())

    @pl.when(jnp.logical_not(ahead))
    def _():
        for c in range(EARLY_CHUNKS, chunks):
            for r in offsets:
                q_copy(c, r).start()


    for c in range(chunks):
        own_q(c).start()
    @pl.when(jnp.logical_not(second))
    def _():
        make_mask()

    kv_buf[1, :, :, WIDTH:] = jnp.ones((STEPS, block_rows, LANES), kv_buf.dtype)
    logs[...] = jnp.zeros_like(logs)

    scale = WIDTH**-0.5
    exponent = scale * 1.4426950408889634

    def one_head(c, j, finish):
        for tile in range(0, block_rows, QUERY_TILE):
            span = slice(tile, tile + QUERY_TILE)
            query = q_buf[c, span, j * WIDTH : (j + 1) * WIDTH]
            finish(c, j, span, query)

    def fold(query, span, steps, prior=None):
        scores = [
            lax.dot_general(
                query,
                kv_buf[0, step, :, :WIDTH],
                (((1,), (1,)), ((), ())),
                preferred_element_type=jnp.float32,
            )
            + bias[span, step * block_rows : (step + 1) * block_rows]
            for step in steps
        ]
        top = functools.reduce(jnp.maximum, scores)
        top = jnp.max(top, axis=1, keepdims=True)
        mixed = jnp.zeros((QUERY_TILE, 2 * WIDTH), jnp.float32)
        if prior is not None:
            before, mixed = prior
            top = jnp.maximum(top, before)
            mixed = mixed * jnp.exp2((before - top) * exponent)
        for score, step in zip(scores, steps):
            weights = jnp.exp2((score - top) * exponent)
            mixed += jnp.dot(
                weights.astype(jnp.bfloat16),
                kv_buf[1, step],
                preferred_element_type=jnp.float32,
            )
        return top, mixed

    def write(c, j, span, top, mixed):
        total = mixed[:, WIDTH:]
        o_buf[c, span, j * WIDTH : (j + 1) * WIDTH] = (mixed[:, :WIDTH] / total).astype(
            o_buf.dtype
        )
        lane = lax.broadcasted_iota(jnp.int32, (QUERY_TILE, LANES), 1)
        logs[span, :] = jnp.where(
            lane == c * CHUNK_HEADS + j, top * scale + jnp.log(total), logs[span, :]
        )

    def near_part(c, j, span, query):
        top, mixed = fold(query, span, NEAR)
        first_top[c, j, span, :] = jnp.broadcast_to(top, (QUERY_TILE, LANES))
        first_mixed[c, j, span, :] = mixed

    def far_part(c, j, span, query):
        prior = (first_top[c, j, span, :1], first_mixed[c, j, span, :])
        write(c, j, span, *fold(query, span, FAR, prior))

    def whole(c, j, span, query):
        write(c, j, span, *fold(query, span, range(STEPS)))

    def take_queries(c):
        own_q(c).wait()
        for r in offsets:
            q_landing(c, r).wait_recv()

    @pl.when(jnp.logical_not(even))
    def _():
        near_landing(0).wait_recv()
        for r in pieces[:-3]:
            next_copy(both, 1, r).wait_send()
        pl.semaphore_signal(go, inc=1, device_id=partner, device_id_type=MESH)
        for r in pieces[-3:]:
            next_copy(both, 1, r).wait_send()

    @pl.when(even)
    def _():
        pl.semaphore_wait(go, 1)

        @pl.when(jnp.logical_not(wraps))
        def _():
            pl.semaphore_wait(ready, 1)

        block_copy().start()

    for r in pieces:
        outer_landing(r).wait_recv()
    take_queries(0)
    one_head(0, 0, near_part)

    @pl.when(first_cycle)
    def _():
        for j in range(1, CHUNK_HEADS):
            one_head(0, j, near_part)

        def near_chunk(c, carry):
            take_queries(c)
            for j in range(CHUNK_HEADS):
                one_head(c, j, near_part)
            return carry

        lax.fori_loop(1, chunks, near_chunk, 0)


    @pl.when(jnp.logical_not(even))
    def _():
        for r in pieces[1:]:
            near_landing(r).wait_recv()
        for r in pieces:
            far_landing(r).wait_recv()
            relay_copy(r).start()

    @pl.when(even)
    def _():
        for r in pieces:
            relay_landing(r).wait_recv()
        block_copy().wait_recv()

    for j in range(CHUNK_HEADS):
        if j:

            @pl.when(first_cycle)
            def _():
                one_head(0, j, far_part)

            @pl.when(jnp.logical_not(first_cycle))
            def _():
                one_head(0, j, whole)

        else:
            one_head(0, j, far_part)
        own_first(j).start()
        for r in offsets:
            first_copy(j, r).start()

    def one_chunk(c, carry):
        @pl.when(first_cycle)
        def _():
            for j in range(CHUNK_HEADS):
                one_head(c, j, far_part)

        @pl.when(jnp.logical_not(first_cycle))
        def _():
            take_queries(c)
            for j in range(CHUNK_HEADS):
                one_head(c, j, whole)

        own_o(c).start()
        for r in offsets:
            o_copy(c, r).start()
        return carry

    lax.fori_loop(1, chunks, one_chunk, 0)
    log_ref[...] = jnp.transpose(logs[...])[:GROUP]

    for r in pieces:
        if r:
            kv_landing(r).wait_send()
        next_copy(both, 2, r).wait_send()

    @pl.when(even)
    def _():
        for r in pieces:
            next_copy(both, 0, r).wait_send()
        block_copy().wait_send()

    @pl.when(jnp.logical_not(even))
    def _():
        for r in pieces:
            relay_copy(r).wait_send()

    for j in range(CHUNK_HEADS):
        own_first(j).wait()
        for r in offsets:
            first_copy(j, r).wait_send()
            first_landing(j, r).wait_recv()
    for r in offsets:
        q_copy(0, r).wait_send()
    for c in range(1, chunks):
        own_o(c).wait()
        for r in offsets:
            q_copy(c, r).wait_send()
            o_copy(c, r).wait_send()
            o_landing(c, r).wait_recv()


def hand_over(mixed_ref, log_in_ref, out_ref, log_ref, sem):
    part = mixed_ref.shape[0] // HAND_OVER_PARTS
    copies = [pltpu.make_async_copy(log_in_ref, log_ref, sem.at[HAND_OVER_PARTS])]
    for n in range(HAND_OVER_PARTS):
        span = pl.ds(n * part, part)
        copies.append(pltpu.make_async_copy(mixed_ref.at[span], out_ref.at[span], sem.at[n]))
    for copy in copies:
        copy.start()
    for copy in copies:
        copy.wait()


def per_device(queries, keys, values, positions, plan):
    sizes = tuple(lax.axis_size(name) for name in ("head", "inner", "outer"))
    heads = sizes[0]
    rows = queries.shape[0]
    block_rows = rows * heads
    chunks = GROUP // CHUNK_HEADS
    place = positions.reshape(-1, LANES)
    used = plan.T
    anywhere = pl.BlockSpec(memory_space=pl.ANY)
    dma = pltpu.SemaphoreType.DMA
    kind = queries.dtype
    queries, keys, values, place, used = (
        pltpu.with_memory_space_constraint(x, pltpu.HBM)
        for x in (queries, keys, values, place, used)
    )
    results = pl.pallas_call(
        functools.partial(attention_kernel, sizes),
        out_shape=(
            jax.ShapeDtypeStruct(queries.shape, kind),
            jax.ShapeDtypeStruct((GROUP, block_rows), jnp.float32),
        ),
        in_specs=[anywhere] * 5,
        out_specs=(anywhere, pl.BlockSpec(memory_space=pltpu.VMEM)),
        scratch_shapes=[
            pltpu.VMEM((2, STEPS, block_rows, 2 * WIDTH), kind),
            pltpu.VMEM((chunks, block_rows, CHUNK_HEADS * WIDTH), kind),
            pltpu.VMEM((chunks, block_rows, CHUNK_HEADS * WIDTH), kind),
            pltpu.VMEM((block_rows, STEPS * block_rows), jnp.float32),
            pltpu.VMEM((block_rows, LANES), jnp.float32),
            pltpu.VMEM((chunks, CHUNK_HEADS, block_rows, LANES), jnp.float32),
            pltpu.VMEM((chunks, CHUNK_HEADS, block_rows, 2 * WIDTH), jnp.float32),
            pltpu.VMEM(place.shape, jnp.int32),
            pltpu.VMEM(used.shape, jnp.int32),
            dma((4,)),
            dma((heads,)),
            dma((heads,)),
            dma((STEPS - 1, heads)),
            dma((STEPS - 1, heads)),
            dma((heads,)),
            dma((heads,)),
            dma((2,)),
            pltpu.SemaphoreType.REGULAR,
            pltpu.SemaphoreType.REGULAR,
            dma((chunks, heads)),
            dma((chunks, heads)),
            dma((chunks, heads)),
            dma((chunks, heads)),
            dma((CHUNK_HEADS, heads)),
            dma((CHUNK_HEADS, heads)),
        ],
        compiler_params=pltpu.CompilerParams(
            collective_id=0, has_side_effects=True, vmem_limit_bytes=30 * 1024 * 1024
        ),
    )(queries, keys, values, place, used)
    return pl.pallas_call(
        hand_over,
        out_shape=tuple(jax.ShapeDtypeStruct(x.shape, x.dtype) for x in results),
        in_specs=[anywhere] * 2,
        out_specs=(anywhere,) * 2,
        scratch_shapes=[
            dma((HAND_OVER_PARTS + 1,)),
        ],
        compiler_params=pltpu.CompilerParams(vmem_limit_bytes=30 * 1024 * 1024),
    )(*results)


def solution(mesh):
    rows = P(("inner", "outer", "head"), None)
    return jax.shard_map(
        per_device,
        mesh=mesh,
        in_specs=(rows, rows, rows, P(), P()),
        out_specs=(rows, P("head", ("inner", "outer"))),
        check_vma=False,
    )
```
